32 devices in a mesh: dp: 2 (over core), row: 4 (over y, x), col: 4 (over z).
Axes of the slice: x: 2, y: 2, z: 4, core: 2. Of those that a mesh axis runs over, the one named last changes fastest.
Arguments:
- hidden: bfloat16 [2048, 1024], P(('dp', 'row')), may hold values from -6 to 6
- segments: int32 [2, 1024], P('dp'), may hold values from 0 to 3, never falling along the last dimension, each value on 1 to 512 neighbouring positions
- cotangent: bfloat16 [2048, 1024], P(('dp', 'row')), may hold values from -6 to 6
- norm_gain: float32 [2, 1024], replicated, may hold values from 0.5 to 1.5
- zx_weight: bfloat16 [2, 1024, 4096], P(None, 'col', 'row'), may hold values from -0.1875 to 0.1875
- dt_weight: bfloat16 [2, 1024, 32], P(None, 'col', 'row'), may hold values from -0.1875 to 0.1875
- bc_weight: bfloat16 [2, 1024, 256], replicated, may hold values from -0.1875 to 0.1875
- conv_x: float32 [2, 4, 2048], P(None, None, ('row', 'col')), may hold values from -3 to 3
- conv_x_bias: float32 [2, 2048], P(None, ('row', 'col')), may hold values from -3 to 3
- conv_bc: float32 [2, 4, 256], replicated, may hold values from -3 to 3
- conv_bc_bias: float32 [2, 256], replicated, may hold values from -3 to 3
- dt_bias: float32 [2, 32], P(None, ('row', 'col')), may hold values from -6 to -2
- a_log: float32 [2, 32], P(None, ('row', 'col')), may hold values from -2 to 2.5
- skip_d: float32 [2, 32], P(None, ('row', 'col')), may hold values from 0.5 to 1.5
- gnorm_gain: float32 [2, 2048], P(None, ('row', 'col')), may hold values from 0.5 to 1.5
- out_weight: bfloat16 [2, 2048, 1024], P(None, ('row', 'col')), may hold values from -0.125 to 0.125
Outputs:
- hidden_out: bfloat16 [2048, 1024], P(('dp', 'row'))
- d_hidden: float32 [2048, 1024], P(('dp', 'row'))
- d_norm_gain: float32 [2, 1024], replicated
- d_zx_weight: float32 [2, 1024, 4096], P(None, 'col', 'row')
- d_dt_weight: float32 [2, 1024, 32], P(None, 'col', 'row')
- d_bc_weight: float32 [2, 1024, 256], replicated
- d_conv_x: float32 [2, 4, 2048], P(None, None, ('row', 'col'))
- d_conv_x_bias: float32 [2, 2048], P(None, ('row', 'col'))
- d_conv_bc: float32 [2, 4, 256], replicated
- d_conv_bc_bias: float32 [2, 256], replicated
- d_dt_bias: float32 [2, 32], P(None, ('row', 'col'))
- d_a_log: float32 [2, 32], P(None, ('row', 'col'))
- d_skip_d: float32 [2, 32], P(None, ('row', 'col'))
- d_gnorm_gain: float32 [2, 2048], P(None, ('row', 'col'))
- d_out_weight: float32 [2, 2048, 1024], P(None, ('row', 'col'))
The draws below stay inside these ranges and needn't reach their ends.
Inputs may be any that keep to these rules, and one draw needn't show every extreme that they name: `segments`: within a sequence the document numbers never fall; each document is a run of 1 to 512 tokens, and in every sequence one document has exactly 512 tokens.
All inputs are finite; a program needn't handle non-finite values.
Results may differ from the reference program's by a relative error of at most 0.04.
Values may be sent and summed in bfloat16 or wider, within the bound.
No kernel may reach another device: no remote copies, remote signals or barrier semaphores. Data moves between devices by JAX's collectives and lax.ppermute only.
A program may use at most 128 MiB of HBM per device.

```python
import math
import jax
import jax.numpy as jnp
import numpy as np
from jax import lax

D = 1024
HEADS = 32
HEAD_DIM = 64
STATE = 128
CONV = 4
LEN = 1024
LAYERS = 2
DOCS = 4
INNER = 2048
SEQUENCES = 2
TOKENS = 2048


def shard_levels(stream_key, extent, cuts, least, largest):
    def one(axis_at, blocks):
        steps = jax.random.uniform(jax.random.fold_in(jax.random.fold_in(stream_key, 6), axis_at), (blocks,), jnp.float32, least / len(cuts), largest / len(cuts))
        return jnp.repeat(jnp.exp(steps), extent[axis_at] // blocks).reshape((-1,) + (1,) * (len(extent) - axis_at - 1))

    gain = one(*cuts[0])
    for cut in cuts[1:]:
        gain = gain * one(*cut)
    return gain


def length_profile(amount, total, reach, skew):
    weights = [(1 << 20) // math.isqrt(grade ** skew) + 1 for grade in range(2, amount + 1)]
    spare, given = total - reach - (amount - 1), [1] * (amount - 1)
    while spare > 0:
        free = [i for i in range(amount - 1) if given[i] < reach]
        whole, budget = sum([weights[i] for i in free]), spare
        for i in free:
            more = min(reach - given[i], max(1, budget * weights[i] // whole), spare)
            given[i] = given[i] + more
            spare = spare - more
    return np.array([reach] + given)


def uneven_parts(own_key, count, total, reach, slope):
    if count == 2:
        one = jax.random.randint(own_key, (), max(1, total - reach), min(reach, total - 1) + 1)
        return jnp.stack([one, total - one])
    sizes = jnp.asarray(length_profile(count, total, reach, slope), jnp.int32)
    pairs = (count - 1) // 2
    source_of, receiver = sizes[1:1 + 2 * pairs:2], sizes[2:2 + 2 * pairs:2]
    room = jnp.minimum(source_of - 1, reach - receiver)
    moved = jax.random.randint(jax.random.fold_in(own_key, 1), (pairs,), 0, 1 << 20) % (room + 1)
    sizes = sizes.at[1:1 + 2 * pairs:2].set(source_of - moved).at[2:2 + 2 * pairs:2].set(receiver + moved)
    return sizes[jax.random.permutation(jax.random.fold_in(own_key, 2), count)]


def normal_values(own_key, shape, deviation, reach, cuts=(), kind=jnp.bfloat16):
    entries = jax.random.normal(own_key, shape, jnp.float32) * deviation
    if len(cuts) > 0:
        entries = shard_levels(own_key, shape, cuts, -0.22, 0.18) * entries
    return jnp.clip(entries, min=-reach, max=reach).astype(kind)


def setup_inputs(seed: int = 0) -> dict:
    seeds = jax.random.split(jax.random.key(seed), 17)
    hidden = normal_values(seeds[0], (TOKENS, D), 1.0, 6.0, ((0, 8),))
    segments = jax.vmap(lambda own: jnp.searchsorted(jnp.cumsum(uneven_parts(own, DOCS, LEN, LEN // 2, 0)), jnp.arange(LEN), side="right"))(jax.random.split(seeds[1], SEQUENCES)).reshape((SEQUENCES, LEN)).astype(jnp.int32)
    cotangent = normal_values(seeds[2], (TOKENS, D), 1.0, 6.0, ((0, 8),))
    norm_gain = jnp.clip(1.0 + 0.1 * jax.random.normal(seeds[3], (LAYERS, D), jnp.float32), 0.5, 1.5)
    zx_weight = normal_values(seeds[4], (LAYERS, D, 2 * INNER), D ** -0.5, 0.1875, ((1, 4), (2, 4)))
    dt_weight = normal_values(seeds[5], (LAYERS, D, HEADS), D ** -0.5, 0.1875, ((1, 4), (2, 4)))
    bc_weight = normal_values(seeds[6], (LAYERS, D, 2 * STATE), D ** -0.5, 0.1875)
    conv_x = normal_values(seeds[7], (LAYERS, CONV, INNER), CONV ** -0.5, 3.0, ((2, 16),), jnp.float32)
    conv_x_bias = normal_values(seeds[8], (LAYERS, INNER), 0.5, 3.0, ((1, 16),), jnp.float32)
    conv_bc = normal_values(seeds[9], (LAYERS, CONV, 2 * STATE), CONV ** -0.5, 3.0, (), jnp.float32)
    conv_bc_bias = normal_values(seeds[10], (LAYERS, 2 * STATE), 0.5, 3.0, (), jnp.float32)
    dt_bias = jnp.clip(-6.0 + 4.0 * jax.random.uniform(seeds[11], (LAYERS, HEADS), jnp.float32) ** shard_levels(seeds[11], (LAYERS, HEADS), ((1, 16),), -0.2, 0.2), -6.0, -2.0)
    a_log = jnp.clip(-2.0 + 4.5 * jax.random.uniform(seeds[12], (LAYERS, HEADS), jnp.float32) ** shard_levels(seeds[12], (LAYERS, HEADS), ((1, 16),), -0.2, 0.2), -2.0, 2.5)
    skip_d = jnp.clip(0.5 + 1.0 * jax.random.uniform(seeds[13], (LAYERS, HEADS), jnp.float32) ** shard_levels(seeds[13], (LAYERS, HEADS), ((1, 16),), -0.2, 0.2), 0.5, 1.5)
    gnorm_gain = jnp.clip(1.0 + 0.1 * jax.random.normal(seeds[14], (LAYERS, INNER), jnp.float32), 0.5, 1.5)
    out_weight = normal_values(seeds[15], (LAYERS, INNER, D), INNER ** -0.5, 0.125, ((1, 16),))
    return {"hidden": hidden, "segments": segments, "cotangent": cotangent, "norm_gain": norm_gain, "zx_weight": zx_weight, "dt_weight": dt_weight, "bc_weight": bc_weight, "conv_x": conv_x, "conv_x_bias": conv_x_bias, "conv_bc": conv_bc, "conv_bc_bias": conv_bc_bias, "dt_bias": dt_bias, "a_log": a_log, "skip_d": skip_d, "gnorm_gain": gnorm_gain, "out_weight": out_weight}


@jax.custom_vjp
def low(v):
    return lax.optimization_barrier(v.astype(jnp.bfloat16)).astype(jnp.float32)

@jax.custom_vjp
def low_back(v):
    return v

def low_keep(v):
    return (low(v), None)

def low_pass(kept, grad):
    return (grad,)

def back_keep(v):
    return (v, None)

def back_low(kept, grad):
    return (low(grad),)
low.defvjp(low_keep, low_pass)
low_back.defvjp(back_keep, back_low)
EPS = 1e-05
HIGHEST = lax.Precision.HIGHEST

def exact_dot(left, right):
    return jnp.dot(left, right, precision=HIGHEST, preferred_element_type=jnp.float32)

def conv_masks(seg_ids):
    seg_masks = [jnp.ones(seg_ids.shape, jnp.float32)]
    for offset in range(1, CONV):
        earlier = jnp.concatenate([jnp.full((offset,), -1, jnp.int32), seg_ids[:-offset]], axis=0)
        seg_masks.append((earlier == seg_ids).astype(jnp.float32))
    return seg_masks

def causal_conv(values, kernel, conv_bias, seg_masks):
    running = conv_bias + kernel[0] * values
    for offset in range(1, kernel.shape[0]):
        padding = jnp.zeros((offset, values.shape[1]), jnp.float32)
        shifted = jnp.concatenate([padding, values[:-offset]], axis=0)
        running = running + kernel[offset] * shifted * seg_masks[offset][:, None]
    return running

def seq_mixer(mixed_in, step_in, side_in, seg_ids, conv_x, conv_x_bias, conv_bc, conv_bc_bias, dt_bias, a_log, skip_d):
    length = seg_ids.shape[0]
    halves = mixed_in.reshape(length, HEADS, 2, HEAD_DIM)
    gate_in = halves[:, :, 0, :]
    values = halves[:, :, 1, :].reshape(length, HEADS * HEAD_DIM)
    seg_masks = conv_masks(seg_ids)
    sources = jax.nn.silu(causal_conv(values, conv_x, conv_x_bias, seg_masks)).reshape(length, HEADS, HEAD_DIM)
    side = jax.nn.silu(causal_conv(side_in, conv_bc, conv_bc_bias, seg_masks))
    inputs = side[:, :STATE]
    readout = side[:, STATE:]
    steps = jax.nn.softplus(step_in + dt_bias)
    decays = jnp.cumsum(steps * -jnp.exp(a_log), axis=0)
    places = jnp.arange(length)
    allowed = (places[:, None] >= places[None, :]) & (seg_ids[:, None] == seg_ids[None, :])
    affinity = exact_dot(readout, inputs.T)

    def one_head(head_args):
        head_src, head_decay, head_step, head_skip = head_args
        spans = head_decay[:, None] - head_decay[None, :]
        weights = affinity * jnp.exp(jnp.where(allowed, spans, -1e+30)) * head_step[None, :]
        return exact_dot(weights, head_src) + head_skip * head_src
    mixed = lax.map(jax.checkpoint(one_head), (sources.transpose(1, 0, 2), decays.T, steps.T, skip_d))
    gated = mixed.transpose(1, 0, 2) * jax.nn.silu(gate_in)
    return gated.reshape(length, HEADS * HEAD_DIM)

def layer_forward(resid, segments, weights):
    norm_gain, zx_weight, dt_weight, bc_weight, conv_x, conv_x_bias, conv_bc, conv_bc_bias, dt_bias, a_log, skip_d, gnorm_gain, out_weight = weights
    scale = lax.rsqrt(lax.optimization_barrier(jnp.mean(resid * resid, axis=1, keepdims=True)) + EPS)
    normed = low(resid * scale * norm_gain)
    mixed_in = low_back(low(exact_dot(normed, zx_weight)))
    step_in = low_back(low(exact_dot(normed, dt_weight)))
    side_in = low_back(low(exact_dot(normed, bc_weight)))
    seq_count = segments.shape[0]
    length = segments.shape[1]

    def one_seq(seq_args):
        seq_mixed, seq_step, seq_side, seq_ids = seq_args
        return seq_mixer(seq_mixed, seq_step, seq_side, seq_ids, conv_x, conv_x_bias, conv_bc, conv_bc_bias, dt_bias, a_log, skip_d)
    gated = lax.map(jax.checkpoint(one_seq), (mixed_in.reshape(seq_count, length, -1), step_in.reshape(seq_count, length, -1), side_in.reshape(seq_count, length, -1), segments))
    gated = gated.reshape(resid.shape[0], HEADS * HEAD_DIM)
    inverse = lax.rsqrt(lax.optimization_barrier(jnp.mean(gated * gated, axis=1, keepdims=True)) + EPS)
    normed_out = low(gated * inverse * gnorm_gain)
    return resid + low_back(exact_dot(normed_out, out_weight))

def reference(hidden, segments, cotangent, norm_gain, zx_weight, dt_weight, bc_weight, conv_x, conv_x_bias, conv_bc, conv_bc_bias, dt_bias, a_log, skip_d, gnorm_gain, out_weight):
    params = (norm_gain, zx_weight.astype(jnp.float32), dt_weight.astype(jnp.float32), bc_weight.astype(jnp.float32), conv_x, conv_x_bias, conv_bc, conv_bc_bias, dt_bias, a_log, skip_d, gnorm_gain, out_weight.astype(jnp.float32))

    def forward(resid, weights):
        for index in range(LAYERS):
            resid = layer_forward(resid, segments, tuple((member[index] for member in weights)))
        return resid
    final, pullback = jax.vjp(forward, hidden.astype(jnp.float32), params)
    grad_hidden, grads = pullback(cotangent.astype(jnp.float32))
    return (final.astype(jnp.bfloat16), grad_hidden, grads[0], grads[1], grads[2], grads[3], grads[4], grads[5], grads[6], grads[7], grads[8], grads[9], grads[10], grads[11], grads[12])
```

```python
import jax
import jax.numpy as jnp
from jax import lax
from jax.experimental import pallas as pl
from jax.experimental.pallas import tpu as pltpu
from jax.sharding import PartitionSpec as P

EPS = 1e-05
BF = jnp.bfloat16
F32 = jnp.float32
HEAD_DIM = 64
STATE = 128
LANES = 128
NN = (((1,), (0,)), ((), ()))
NT = (((1,), (1,)), ((), ()))
TN = (((0,), (0,)), ((), ()))
VMEM_BYTES = 58 * 1024 * 1024


def dot(left, right, dims=NN):
    return lax.dot_general(left, right, dims, preferred_element_type=F32)


def shape(dims, dtype):
    return jax.ShapeDtypeStruct(dims, dtype)


def local_call(body, outs, scalars, arrays, scratch=(), name=None):
    smem = pl.BlockSpec(memory_space=pltpu.SMEM)
    vmem = pl.BlockSpec(memory_space=pltpu.VMEM)
    return pl.pallas_call(
        body,
        out_shape=tuple(outs),
        in_specs=[smem] * len(scalars) + [vmem] * len(arrays),
        out_specs=tuple(vmem for _ in outs),
        scratch_shapes=list(scratch),
        compiler_params=pltpu.CompilerParams(vmem_limit_bytes=VMEM_BYTES),
        name=name,
    )(*scalars, *arrays)


def row_peer(index, step):
    return index ^ step


def col_dest(index, step):
    return lax.rem(index + step, 4)


def col_source(index, step):
    return lax.rem(index + 4 - step, 4)


def block(index, size):
    return pl.ds(pl.multiple_of(index * size, size), size)


def across_rows(pieces):
    return [pieces[0]] + [
        lax.ppermute(pieces[step], "row", [(i, i ^ step) for i in range(4)]) for step in range(1, 4)
    ]


def across_cols(pieces):
    return [pieces[0]] + [
        lax.ppermute(pieces[step], "col", [(i, (i + step) % 4) for i in range(4)])
        for step in range(1, 4)
    ]


def pair_swap(array):
    count = lax.axis_size("dp")
    return lax.ppermute(array, "dp", [(i, i ^ 1) for i in range(count)])


def copies_sum(array):
    if lax.axis_size("dp") > 2:
        return lax.psum(array, "dp").astype(F32)
    return array.astype(F32) + pair_swap(array).astype(F32)


def split_wide(value, rows):
    high = value.astype(BF).astype(F32)
    lane = lax.broadcasted_iota(jnp.int32, (rows, LANES), 1)
    return jnp.where(lane < 64, high, value - high)


def join_wide(lanes):
    return lanes[:, 0:1] + lanes[:, 64:65]


def start_body(tokens_ref, gain_ref, resid_ref, normed_ref, scale_ref):
    resid = tokens_ref[...].astype(F32)
    width = resid.shape[1]
    scale = lax.rsqrt(jnp.sum(resid * resid, axis=1, keepdims=True) / width + EPS)
    resid_ref[...] = resid
    normed_ref[...] = (resid * scale * gain_ref[...]).astype(BF)
    scale_ref[...] = jnp.broadcast_to(scale, scale_ref.shape)


def collect_branch(own_ref, others, inner):
    total = own_ref[...]
    for other in others:
        total = total + other[...].astype(F32)
    width = total.shape[1] - LANES
    inverse = lax.rsqrt(join_wide(total[:, width:]) / inner + EPS)
    return total[:, :width], inverse


def middle_body(inner, own, one, two, three, resid_ref, gain_ref, next_ref, mixed_ref, inv_ref,
                normed_ref, scale_ref):
    mixed, inverse = collect_branch(own, (one, two, three), inner)
    resid = resid_ref[...] + inverse * mixed
    width = resid.shape[1]
    scale = lax.rsqrt(jnp.sum(resid * resid, axis=1, keepdims=True) / width + EPS)
    next_ref[...] = resid
    mixed_ref[...] = mixed
    inv_ref[...] = jnp.broadcast_to(inverse, inv_ref.shape)
    normed_ref[...] = (resid * scale * gain_ref[...]).astype(BF)
    scale_ref[...] = jnp.broadcast_to(scale, scale_ref.shape)


def send_grad(grad, mixed, inverse, inner, out_ref):
    rows, width = grad.shape
    scaled = (grad * inverse).astype(BF)
    along = jnp.sum(scaled.astype(F32) * mixed, axis=1, keepdims=True)
    factor = inverse * inverse * along / inner
    out_ref[:, :width] = scaled
    out_ref[:, width:] = split_wide(factor, rows).astype(BF)


def turn_body(inner, own, one, two, three, resid_ref, cot_ref, result_ref, sent_ref):
    mixed, inverse = collect_branch(own, (one, two, three), inner)
    result_ref[...] = (resid_ref[...] + inverse * mixed).astype(BF)
    send_grad(cot_ref[...].astype(F32), mixed, inverse, inner, sent_ref)


def norm_back(own, others, grad, resid, scale, gain):
    total = own[...]
    for other in others:
        total = total + other[...].astype(F32)
    weighted = total * gain
    width = resid.shape[1]
    along = jnp.sum(resid * weighted, axis=1, keepdims=True)
    return grad + scale * weighted - resid * (scale * scale * scale * along / width)


def back_middle_body(inner, own, one, two, three, grad_ref, resid_ref, scale_ref, gain_ref,
                     mixed_ref, inv_ref, out_ref, sent_ref):
    grad = norm_back(own, (one, two, three), grad_ref[...].astype(F32), resid_ref[...],
                     scale_ref[:, 0:1], gain_ref[...])
    out_ref[...] = grad
    send_grad(grad, mixed_ref[...], inv_ref[:, 0:1], inner, sent_ref)


def back_end_body(own, one, two, three, grad_ref, resid_ref, scale_ref, gain_ref, out_ref):
    grad = norm_back(own, (one, two, three), grad_ref[...], resid_ref[...], scale_ref[:, 0:1],
                     gain_ref[...])
    out_ref[...] = grad.astype(BF)


def place_body(place_ref, a0, a1, a2, a3, b0, b1, b2, b3, low_ref, wide_ref):
    col = place_ref[1]
    for step, (low, wide) in enumerate(((a0, b0), (a1, b1), (a2, b2), (a3, b3))):
        rows = block(col_source(col, step), low.shape[0])
        low_ref[rows, :] = low[...]
        wide_ref[rows, :] = wide[...].astype(F32)


def project_in_body(place_ref, x0, x1, x2, x3, mine_ref, other_ref, side_ref, normed_ref,
                    m0, m1, m2, m3):
    row, col, half = place_ref[0], place_ref[1], place_ref[2]
    for step, piece in enumerate((x0, x1, x2, x3)):
        normed_ref[block(row_peer(row, step), 64), :] = piece[...]
    mine = jnp.concatenate([normed_ref[:, block(2 * j + half, 128)] for j in range(4)], axis=1)
    other = jnp.concatenate([normed_ref[:, block(2 * j + 1 - half, 128)] for j in range(4)], axis=1)
    side = dot(normed_ref[...], side_ref[...]).astype(BF)
    width = mine_ref.shape[1] - LANES
    steps = dot(mine, mine_ref[:, width:]) + dot(other, other_ref[:, width:])
    steps = steps.astype(BF).astype(F32).T[0:16, :].astype(BF)
    for step, out in enumerate((m0, m1, m2, m3)):
        cols = block(col_dest(col, step), 256)
        value = dot(mine, mine_ref[:, cols]) + dot(other, other_ref[:, cols])
        out[0:256, 0:256] = value.astype(BF)
        out[0:256, 256:512] = side
        out[256:272, 0:256] = steps
        out[256:272, 256:512] = jnp.zeros((16, 256), BF)


def sigmoid(value):
    return 1.0 / (1.0 + jnp.exp(-value))


def lane_scan(value):
    length = value.shape[1]
    lane = lax.broadcasted_iota(jnp.int32, value.shape, 1)
    step = 1
    while step < length:
        value = value + jnp.where(lane >= step, pltpu.roll(value, step, 1), 0.0)
        step *= 2
    return value


def lane_scan_back(value):
    length = value.shape[1]
    lane = lax.broadcasted_iota(jnp.int32, value.shape, 1)
    step = 1
    while step < length:
        value = value + jnp.where(
            lane < length - step, pltpu.roll(value, length - step, 1), 0.0
        )
        step *= 2
    return value


def gather_sequence(col, pieces, zx_s, bc_s, dt_s):
    for step, piece in enumerate(pieces):
        at = col_source(col, step)
        zx_s[block(at, 256), :] = piece[0:256, 0:256]
        bc_s[block(at, 256), :] = piece[0:256, 256:512]
        dt_s[:, block(at, 256)] = piece[256:272, 0:256].astype(F32)


def step_rows(col, dt_s, params):
    raw = dt_s[...]
    at = lax.broadcasted_iota(jnp.int32, raw.shape, 0)
    first = jnp.sum(jnp.where(at == 2 * col, raw, 0.0), axis=0, keepdims=True) + params[0]
    second = jnp.sum(jnp.where(at == 2 * col + 1, raw, 0.0), axis=0, keepdims=True) + params[1]
    at8 = lax.broadcasted_iota(jnp.int32, (8, raw.shape[1]), 0)
    pre = jnp.where(at8 == 0, first, second)
    steps = jnp.maximum(pre, 0.0) + jnp.log1p(jnp.exp(-jnp.abs(pre)))
    rate = jnp.where(at8 == 0, params[2], params[3])
    return pre, steps, rate, lane_scan(steps * rate)


def conv_pre(values, taps, masks_ref):
    total = taps[4:5, :] + taps[0:1, :] * values
    for offset in range(1, 4):
        moved = pltpu.roll(values, offset, 0) * masks_ref[:, offset:offset + 1]
        total = total + taps[offset:offset + 1, :] * moved
    return total


def head_pre(head, zx_s, taps_ref, masks_ref):
    values = zx_s[:, head * 128:head * 128 + 128].astype(F32)
    lane = lax.broadcasted_iota(jnp.int32, values.shape, 1)
    conv = conv_pre(values, taps_ref[head * 8:head * 8 + 8, :], masks_ref)
    return values, jnp.where(lane < 64, values, conv)


def reach(i, j, masks_ref, seg_ref):
    same = masks_ref[i * 256:i * 256 + 256, 0:1] == seg_ref[0:1, j * 256:j * 256 + 256]
    if i == j:
        at = lax.broadcasted_iota(jnp.int32, (256, 256), 0)
        to = lax.broadcasted_iota(jnp.int32, (256, 256), 1)
        same = same & (at >= to)
    return same


def pairs():
    return [(i, j) for i in range(4) for j in range(max(0, i - 2), i + 1)]


def mix_body(place_ref, params, m0, m1, m2, m3, masks_ref, seg_ref, taps_ref, side_taps_ref,
             y_ref, g0, g1, g2, g3, zx_s, bc_s, dt_s, src_s, src_low, b_s, c_s, row_s, col_s, acc_s,
             g_s):
    col = place_ref[1]
    gather_sequence(col, (m0, m1, m2, m3), zx_s, bc_s, dt_s)
    pre, steps, rate, cum = step_rows(col, dt_s, params)
    row_s[0:8, :] = steps
    row_s[8:16, :] = cum
    col_s[...] = jnp.concatenate([cum, jnp.zeros((120, cum.shape[1]), F32)], axis=0).T
    for head in range(2):
        values, active = head_pre(head, zx_s, taps_ref, masks_ref)
        active = active * sigmoid(active)
        src_s[:, head * 128:head * 128 + 128] = active
        src_low[:, head * 128:head * 128 + 128] = active.astype(BF)
    for part, out in enumerate((b_s, c_s)):
        lanes = slice(part * 128, part * 128 + 128)
        conv = conv_pre(bc_s[:, lanes].astype(F32), side_taps_ref[:, lanes], masks_ref)
        out[...] = (conv * sigmoid(conv)).astype(BF)
    acc_s[...] = jnp.zeros_like(acc_s)
    for i, j in pairs():
        ri, rj = slice(i * 256, i * 256 + 256), slice(j * 256, j * 256 + 256)
        affinity = dot(c_s[ri, :], b_s[rj, :], NT)
        allowed = reach(i, j, masks_ref, seg_ref)
        for head in range(2):
            lanes = slice(head * 128, head * 128 + 128)
            span = col_s[ri, head:head + 1] - row_s[8 + head:9 + head, rj]
            weight = jnp.exp(jnp.where(allowed, span, -1e30)) * affinity * row_s[head:head + 1, rj]
            acc_s[ri, lanes] += dot(weight.astype(BF), src_low[rj, lanes])
    lane = lax.broadcasted_iota(jnp.int32, (1024, 128), 1)
    y0 = acc_s[:, 0:128] + params[4] * src_s[:, 0:128]
    y1 = acc_s[:, 128:256] + params[5] * src_s[:, 128:256]
    y = jnp.where(lane < 64, pltpu.roll(y0, 64, 1), y1)
    gate = jnp.where(lane < 64, src_s[:, 0:128], pltpu.roll(src_s[:, 128:256], 64, 1))
    y_ref[...] = y
    g_s[...] = (y * gate).astype(BF)
    for step, out in enumerate((g0, g1, g2, g3)):
        out[...] = g_s[block(col_dest(col, step), 256), :]


def mix_back_body(place_ref, params, d0, d1, d2, d3, m0, m1, m2, m3, y_ref, masks_ref, seg_ref,
                  taps_ref, side_taps_ref, o0, o1, o2, o3, head_ref, side_ref, small_ref,
                  zx_s, bc_s, dt_s, src_s, src_low, slope_s, bc_low, bc_slope, row_s, col_s,
                  dy_s, dy_low, dgy_s, dsrc_s, dbc_s, rows_s, cols_s, dg_s, out_zx, out_bc, out_dt):
    col = place_ref[1]
    gather_sequence(col, (m0, m1, m2, m3), zx_s, bc_s, dt_s)
    for step, piece in enumerate((d0, d1, d2, d3)):
        dg_s[block(col_source(col, step), 256), :] = piece[...].astype(F32)
    pre, steps, rate, cum = step_rows(col, dt_s, params)
    row_s[0:8, :] = steps
    row_s[8:16, :] = cum
    col_s[...] = jnp.concatenate([cum, jnp.zeros((120, cum.shape[1]), F32)], axis=0).T
    lane = lax.broadcasted_iota(jnp.int32, (1024, 128), 1)
    skips = []
    for head in range(2):
        lanes = slice(head * 128, head * 128 + 128)
        values, active = head_pre(head, zx_s, taps_ref, masks_ref)
        sig = sigmoid(active)
        source = active * sig
        slope = sig * (1.0 + active * (1.0 - sig))
        src_low[:, lanes] = source.astype(BF)
        slope_s[:, lanes] = slope
        grad = dg_s[...] if head == 0 else pltpu.roll(dg_s[...], 64, 1)
        y = y_ref[...] if head == 0 else pltpu.roll(y_ref[...], 64, 1)
        dgy_s[:, lanes] = grad * y * slope
        dy = jnp.where(lane < 64, 0.0, pltpu.roll(grad * source, 64, 1))
        dy_low[:, lanes] = dy.astype(BF)
        dsrc_s[:, lanes] = params[4 + head] * dy
        skips.append(jnp.sum(dy * source))
    for part in range(2):
        lanes = slice(part * 128, part * 128 + 128)
        conv = conv_pre(bc_s[:, lanes].astype(F32), side_taps_ref[:, lanes], masks_ref)
        sig = sigmoid(conv)
        bc_low[:, lanes] = (conv * sig).astype(BF)
        bc_slope[:, lanes] = sig * (1.0 + conv * (1.0 - sig))
    dbc_s[...] = jnp.zeros_like(dbc_s)
    rows_s[...] = jnp.zeros_like(rows_s)
    cols_s[...] = jnp.zeros_like(cols_s)
    lane256 = lax.broadcasted_iota(jnp.int32, (256, 128), 1)
    for i, j in pairs():
        ri, rj = slice(i * 256, i * 256 + 256), slice(j * 256, j * 256 + 256)
        affinity = dot(bc_low[ri, 128:256], bc_low[rj, 0:128], NT)
        allowed = reach(i, j, masks_ref, seg_ref)
        shared = None
        for head in range(2):
            lanes = slice(head * 128, head * 128 + 128)
            span = col_s[ri, head:head + 1] - row_s[8 + head:9 + head, rj]
            decay = jnp.exp(jnp.where(allowed, span, -1e30))
            step = row_s[head:head + 1, rj]
            inner = dot(dy_low[ri, lanes], src_low[rj, lanes], NT)
            weight = (decay * affinity * step).astype(BF)
            dsrc_s[rj, lanes] += dot(weight, dy_low[ri, lanes], TN)
            both = decay * inner
            term = both * step
            shared = term if shared is None else shared + term
            product = affinity * both
            cols_s[head:head + 1, rj] += jnp.sum(product, axis=0, keepdims=True)
            total = jnp.sum(affinity * term, axis=1, keepdims=True)
            rows_s[ri, :] += jnp.where(lane256 == head, total, 0.0)
        low = shared.astype(BF)
        dbc_s[ri, 128:256] += dot(low, bc_low[rj, 0:128])
        dbc_s[rj, 0:128] += dot(low, bc_low[ri, 128:256], TN)
    sums = rows_s[...].T[0:8, :]
    col_sum = cols_s[...]
    back = lane_scan_back(sums - col_sum * steps)
    dstep = col_sum + rate * back
    at8 = lax.broadcasted_iota(jnp.int32, steps.shape, 0)
    dlog = rate * jnp.sum(steps * back, axis=1, keepdims=True)
    draw = dstep * sigmoid(pre)
    dbias = jnp.sum(draw, axis=1, keepdims=True)
    lane8 = lax.broadcasted_iota(jnp.int32, (8, 128), 1)
    row8 = lax.broadcasted_iota(jnp.int32, (8, 128), 0)
    dskip = jnp.where(row8 == 0, skips[0], skips[1])
    small_ref[...] = jnp.where(
        lane8 == 0, dbias, jnp.where(lane8 == 1, dlog[:, 0:1], jnp.where(lane8 == 2, dskip, 0.0))
    )
    at16 = lax.broadcasted_iota(jnp.int32, (16, 1024), 0)
    out_dt[...] = jnp.where(
        at16 == 2 * col, draw[0:1, :], jnp.where(at16 == 2 * col + 1, draw[1:2, :], 0.0)
    ).astype(BF)

    def conv_back(values, du, taps, out_ref, rows, lanes):
        dv = taps[0:1, :] * du
        out_ref[rows:rows + 1, lanes] = jnp.sum(du * values, axis=0, keepdims=True)
        for offset in range(1, 4):
            masked = du * masks_ref[:, offset:offset + 1]
            out_ref[rows + offset:rows + offset + 1, lanes] = jnp.sum(
                masked * pltpu.roll(values, offset, 0), axis=0, keepdims=True
            )
            dv = dv + taps[offset:offset + 1, :] * pltpu.roll(masked, 1024 - offset, 0)
        out_ref[rows + 4:rows + 5, lanes] = jnp.sum(du, axis=0, keepdims=True)
        return dv

    head_ref[...] = jnp.zeros_like(head_ref)
    side_ref[...] = jnp.zeros_like(side_ref)
    for head in range(2):
        lanes = slice(head * 128, head * 128 + 128)
        values = zx_s[:, lanes].astype(F32)
        du = jnp.where(lane < 64, 0.0, dsrc_s[:, lanes] * slope_s[:, lanes])
        taps = taps_ref[head * 8:head * 8 + 8, :]
        dv = conv_back(values, du, taps, head_ref, head * 8, slice(0, 128))
        out_zx[:, lanes] = jnp.where(lane < 64, dgy_s[:, lanes], dv).astype(BF)
    for part in range(2):
        lanes = slice(part * 128, part * 128 + 128)
        values = bc_s[:, lanes].astype(F32)
        du = dbc_s[:, lanes] * bc_slope[:, lanes]
        dv = conv_back(values, du, side_taps_ref[:, lanes], side_ref, 0, lanes)
        out_bc[:, lanes] = dv.astype(BF)
    for step, out in enumerate((o0, o1, o2, o3)):
        at = col_dest(col, step)
        out[0:256, 0:256] = out_zx[block(at, 256), :]
        out[0:256, 256:512] = out_bc[block(at, 256), :]
        out[256:272, 0:256] = out_dt[:, block(at, 256)]
        out[256:272, 256:512] = jnp.zeros((16, 256), BF)


def project_out_body(place_ref, g0, g1, g2, g3, mine_ref, other_ref, full_ref, o0, o1, o2, o3,
                     acc_s):
    row, col, half = place_ref[0], place_ref[1], place_ref[2]
    for step, piece in enumerate((g0, g1, g2, g3)):
        full_ref[:, block(col_source(col, step), 128)] = piece[...]
    full = full_ref[...]
    width = 2 * mine_ref.shape[1]
    acc_s[:, block(half, width // 2)] = dot(full, mine_ref[...])
    acc_s[:, block(1 - half, width // 2)] = dot(full, other_ref[...])
    wide = full.astype(F32)
    acc_s[:, width:] = split_wide(jnp.sum(wide * wide, axis=1, keepdims=True), wide.shape[0])
    for step, out in enumerate((o0, o1, o2, o3)):
        out[...] = acc_s[block(row_peer(row, step), 64), :].astype(out.dtype)


def out_back_body(place_ref, q0, q1, q2, q3, mine_ref, other_ref, full_ref, grad_ref, gain_ref,
                  d0, d1, d2, d3, dg_s, fac_s):
    row, col, half = place_ref[0], place_ref[1], place_ref[2]
    width = grad_ref.shape[1]
    for step, piece in enumerate((q0, q1, q2, q3)):
        rows = block(row_peer(row, step), 64)
        grad_ref[rows, :] = piece[:, 0:width]
        fac_s[rows, :] = piece[:, width:].astype(F32)
    value = dot(grad_ref[:, block(half, width // 2)], mine_ref[...], NT)
    value = value + dot(grad_ref[:, block(1 - half, width // 2)], other_ref[...], NT)
    full = full_ref[...].astype(F32)
    gain_ref[...] = (value * full).astype(BF)
    dg_s[...] = (value - full * join_wide(fac_s[...])).astype(BF)
    for step, out in enumerate((d0, d1, d2, d3)):
        out[...] = dg_s[:, block(col_dest(col, step), 128)]


def out_weight_body(full_ref, grad_ref, gain_ref, out_ref):
    width = grad_ref.shape[1]
    out_ref[:, 0:width] = dot(full_ref[...], grad_ref[...], TN).astype(BF)
    ones = jnp.ones((gain_ref.shape[0], LANES), BF)
    out_ref[:, width:] = dot(gain_ref[...], ones, TN).astype(BF)


def in_back_body(place_ref, d0, d1, d2, d3, mine_ref, other_ref, side_ref, normed_ref,
                 full_ref, dside_ref, gain_ref, o0, o1, o2, o3, dx_s):
    row, col, half = place_ref[0], place_ref[1], place_ref[2]
    pieces = (d0, d1, d2, d3)
    side = None
    steps = None
    for step, piece in enumerate(pieces):
        full_ref[:, block(col_source(col, step), 256)] = piece[0:256, 0:256]
        part = piece[0:256, 256:512].astype(F32)
        more = piece[256:272, 0:256].astype(F32)
        side = part if side is None else side + part
        steps = more if steps is None else steps + more
    dside = side.astype(BF)
    dside_ref[...] = dside
    width = full_ref.shape[1] - LANES
    full_ref[:, width:] = jnp.concatenate([steps, jnp.zeros((112, 256), F32)], axis=0).T.astype(BF)
    full = full_ref[...]
    mine = dot(full, mine_ref[...], NT)
    other = dot(full, other_ref[...], NT)
    for j in range(4):
        dx_s[:, block(2 * j + half, 128)] = mine[:, j * 128:j * 128 + 128]
        dx_s[:, block(2 * j + 1 - half, 128)] = other[:, j * 128:j * 128 + 128]
    dx_s[...] += dot(dside, side_ref[...], NT)
    gains = jnp.sum(dx_s[...] * normed_ref[...].astype(F32), axis=0, keepdims=True)
    gain_ref[...] = jnp.broadcast_to(gains, gain_ref.shape)
    for step, out in enumerate((o0, o1, o2, o3)):
        out[...] = dx_s[block(row_peer(row, step), 64), :].astype(out.dtype)


def in_weight_body(normed_ref, full_ref, dside_ref, out_ref, side_ref):
    normed = normed_ref[...]
    out_ref[...] = dot(normed, full_ref[...], TN).astype(BF)
    side_ref[...] = dot(normed, dside_ref[...], TN).astype(BF)


def whole_sum(array, row):
    total = copies_sum(array).astype(BF)
    rows = array.shape[0] // 4
    mine = [
        lax.dynamic_slice_in_dim(total, (row ^ step) * rows, rows, 0) for step in range(4)
    ]
    got = across_rows(mine)
    part = sum(piece.astype(F32) for piece in got).astype(BF)
    got = across_cols([part] * 4)
    part = sum(piece.astype(F32) for piece in got).astype(BF)
    got = across_rows([part] * 4)
    out = jnp.zeros(array.shape, BF)
    for step in range(4):
        out = lax.dynamic_update_slice_in_dim(out, got[step], (row ^ step) * rows, 0)
    return out.astype(F32)


def shards(
    hidden,
    segments,
    cotangent,
    norm_gain,
    zx_weight,
    dt_weight,
    bc_weight,
    conv_x,
    conv_x_bias,
    conv_bc,
    conv_bc_bias,
    dt_bias,
    a_log,
    skip_d,
    gnorm_gain,
    out_weight,
):
    row, col, copy = lax.axis_index("row"), lax.axis_index("col"), lax.axis_index("dp")
    half = copy % 2
    layers, width = norm_gain.shape
    length = segments.shape[1]
    heads_here = dt_weight.shape[2]
    inner = 4 * 4 * conv_x.shape[2]
    place = jnp.stack([row, col, half, row]).astype(jnp.int32)
    swap = [(i * 4 + j, j * 4 + i) for i in range(4) for j in range(4)]

    tokens = lax.ppermute(
        lax.dynamic_slice_in_dim(hidden, col * 64, 64, 0), ("row", "col"), swap
    )
    cot = lax.ppermute(
        lax.dynamic_slice_in_dim(cotangent, col * 64, 64, 0), ("row", "col"), swap
    )

    def fetch(array):
        mine = lax.all_gather(array, "col", axis=0, tiled=True)
        return mine, pair_swap(mine)

    in_weights, out_weights = [], []
    for layer in range(layers):
        joined = jnp.concatenate(
            [zx_weight[layer], jnp.pad(dt_weight[layer], ((0, 0), (0, LANES - heads_here)))], axis=1
        )
        in_weights.append(fetch(lax.dynamic_slice_in_dim(joined, half * 128, 128, 0)))
        scaled = (gnorm_gain[layer][:, None] * out_weight[layer].astype(F32)).astype(BF)
        out_weights.append(
            fetch(lax.dynamic_slice_in_dim(scaled, half * (width // 2), width // 2, 1))
        )

    seg = segments[0].astype(F32)
    columns = [seg]
    for offset in range(1, 4):
        earlier = jnp.concatenate([jnp.full((offset,), -1.0, F32), seg[:-offset]])
        columns.append((earlier == seg).astype(F32))
    masks = jnp.pad(jnp.stack(columns, axis=1), ((0, 0), (0, LANES - 4)))
    seg_rows = jnp.broadcast_to(seg[None], (8, length))
    taps_x = jnp.concatenate([conv_x, conv_x_bias[:, None]], axis=1).reshape(layers, 5, 2, 64)
    taps_x = jnp.pad(taps_x.transpose(0, 2, 1, 3), ((0, 0), (0, 0), (0, 3), (64, 0)))
    taps_x = taps_x.reshape(layers, 16, LANES)
    taps_bc = jnp.pad(
        jnp.concatenate([conv_bc, conv_bc_bias[:, None]], axis=1), ((0, 0), (0, 3), (0, 0))
    )
    params = jnp.concatenate(
        [dt_bias, -jnp.exp(a_log), skip_d, jnp.zeros_like(skip_d)], axis=1
    )
    gains = norm_gain[:, None]

    wide = width + LANES
    kept = []
    resid, normed, scale = local_call(
        start_body,
        [shape((64, width), F32), shape((64, width), BF), shape((64, LANES), F32)],
        [], [tokens, gains[0]], name="start",
    )
    for layer in range(layers):
        pieces = across_rows([normed] * 4)
        full_normed, *sent = local_call(
            project_in_body,
            [shape((256, width), BF)] + [shape((272, 512), BF)] * 4,
            [place], [*pieces, *in_weights[layer], bc_weight[layer]], name="project_in",
        )
        mixed_in = across_cols(sent)
        y, *sent = local_call(
            mix_body,
            [shape((length, 128), F32)] + [shape((256, 128), BF)] * 4,
            [place, params[layer]],
            [*mixed_in, masks, seg_rows, taps_x[layer], taps_bc[layer]],
            [
                pltpu.VMEM((length, 256), BF),
                pltpu.VMEM((length, 256), BF),
                pltpu.VMEM((16, length), F32),
                pltpu.VMEM((length, 256), F32),
                pltpu.VMEM((length, 256), BF),
                pltpu.VMEM((length, 128), BF),
                pltpu.VMEM((length, 128), BF),
                pltpu.VMEM((16, length), F32),
                pltpu.VMEM((length, 128), F32),
                pltpu.VMEM((length, 256), F32),
                pltpu.VMEM((length, 128), BF),
            ],
            name="mix",
        )
        gated = across_cols(sent)
        full_gated, *sent = local_call(
            project_out_body,
            [shape((256, 512), BF), shape((64, wide), F32)] + [shape((64, wide), BF)] * 3,
            [place], [*gated, *out_weights[layer]],
            [pltpu.VMEM((256, wide), F32)], name="project_out",
        )
        parts = across_rows(sent)
        entry = [resid, scale, full_normed, mixed_in, y, full_gated]
        if layer + 1 < layers:
            resid, mixed, inverse, normed, scale = local_call(
                lambda *refs: middle_body(inner, *refs),
                [shape((64, width), F32), shape((64, width), F32), shape((64, LANES), F32),
                 shape((64, width), BF), shape((64, LANES), F32)],
                [], [*parts, resid, gains[layer + 1]], name="middle",
            )
            entry += [mixed, inverse]
        else:
            result, sent_grad = local_call(
                lambda *refs: turn_body(inner, *refs),
                [shape((64, width), BF), shape((64, wide), BF)],
                [], [*parts, resid, cot], name="turn",
            )
        kept.append(entry)

    grad = cot
    head_out, shared_out = [None] * layers, [None] * layers
    for layer in reversed(range(layers)):
        resid, scale, full_normed, mixed_in, y, full_gated = kept[layer][:6]
        pieces = across_rows([sent_grad] * 4)
        full_grad, gain_terms, *sent = local_call(
            out_back_body,
            [shape((256, width), BF), shape((256, 512), BF)] + [shape((256, 128), BF)] * 4,
            [place], [*pieces, *out_weights[layer], full_gated],
            [pltpu.VMEM((256, 512), BF), pltpu.VMEM((256, LANES), F32)], name="out_back",
        )
        dgated = across_cols(sent)
        (out_grad,) = local_call(
            out_weight_body, [shape((512, wide), BF)], [], [full_gated, full_grad, gain_terms],
            name="out_weight",
        )
        o0, o1, o2, o3, head_grads, side_grads, small_grads = local_call(
            mix_back_body,
            [shape((272, 512), BF)] * 4
            + [shape((16, LANES), F32), shape((8, 256), F32), shape((8, LANES), F32)],
            [place, params[layer]],
            [*dgated, *mixed_in, y, masks, seg_rows, taps_x[layer], taps_bc[layer]],
            [
                pltpu.VMEM((length, 256), BF),
                pltpu.VMEM((length, 256), BF),
                pltpu.VMEM((16, length), F32),
                pltpu.VMEM((length, 256), F32),
                pltpu.VMEM((length, 256), BF),
                pltpu.VMEM((length, 256), F32),
                pltpu.VMEM((length, 256), BF),
                pltpu.VMEM((length, 256), F32),
                pltpu.VMEM((16, length), F32),
                pltpu.VMEM((length, 128), F32),
                pltpu.VMEM((8, 128), F32),
                pltpu.VMEM((length, 256), BF),
                pltpu.VMEM((length, 256), F32),
                pltpu.VMEM((length, 256), F32),
                pltpu.VMEM((length, 256), F32),
                pltpu.VMEM((length, 128), F32),
                pltpu.VMEM((8, length), F32),
                pltpu.VMEM((length, 128), F32),
                pltpu.VMEM((length, 256), BF),
                pltpu.VMEM((length, 256), BF),
                pltpu.VMEM((16, length), BF),
            ],
            name="mix_back",
        )
        dmixed = across_cols([o0, o1, o2, o3])
        full_dzx, full_dside, gain_rows, *sent = local_call(
            in_back_body,
            [shape((256, wide), BF), shape((256, 256), BF), shape((8, width), F32),
             shape((64, width), F32)] + [shape((64, width), BF)] * 3,
            [place], [*dmixed, *in_weights[layer], bc_weight[layer], full_normed],
            [pltpu.VMEM((256, width), F32)], name="in_back",
        )
        parts = across_rows(sent)
        if layer > 0:
            mixed, inverse = kept[layer - 1][6:]
            grad, sent_grad = local_call(
                lambda *refs: back_middle_body(inner, *refs),
                [shape((64, width), F32), shape((64, wide), BF)],
                [], [*parts, grad, resid, scale, gains[layer], mixed, inverse],
                name="back_middle",
            )
        else:
            (final,) = local_call(
                back_end_body, [shape((64, width), BF)],
                [], [*parts, grad, resid, scale, gains[layer]], name="back_end",
            )
        in_grad, side_weight = local_call(
            in_weight_body, [shape((width, wide), BF), shape((width, 256), BF)],
            [], [full_normed, full_dzx, full_dside], name="in_weight",
        )
        in_total = lax.psum_scatter(
            copies_sum(in_grad).astype(BF), "col", scatter_dimension=0, tiled=True
        ).astype(F32)
        out_total = lax.psum_scatter(
            copies_sum(out_grad).astype(BF), "col", scatter_dimension=0, tiled=True
        ).astype(F32)
        small = copies_sum(jnp.concatenate([head_grads, small_grads], axis=0))
        gain_part = (gain_rows[0] / norm_gain[layer]).reshape(4, 256)
        shared = jnp.concatenate(
            [side_weight, jnp.pad(
                jnp.concatenate([gain_part, side_grads[:5]], axis=0), ((0, 55), (0, 0))
            ).astype(BF)], axis=0,
        )
        shared = whole_sum(shared, row)
        taps_grad = small[:16].reshape(2, 8, LANES)[:, :5, 64:].transpose(1, 0, 2).reshape(5, 128)
        own_gain = gnorm_gain[layer]
        head_out[layer] = (
            in_total[:, :width],
            in_total[:, width:width + heads_here],
            taps_grad[:4],
            taps_grad[4],
            small[16:18, 0],
            small[16:18, 1],
            small[16:18, 2],
            out_total[:, width] / own_gain,
            out_total[:, :width] * own_gain[:, None],
        )
        shared_out[layer] = (
            shared[width:width + 4].reshape(width),
            shared[:width],
            shared[width + 4:width + 8],
            shared[width + 8],
        )

    def home(array):
        return across_cols([lax.ppermute(array, ("row", "col"), swap)] * 4)

    result_out, grad_out = local_call(
        place_body, [shape((256, width), BF), shape((256, width), F32)],
        [place], [*home(result), *home(final)], name="place",
    )
    heads = [jnp.stack([head_out[i][k] for i in range(layers)]) for k in range(9)]
    shared = [jnp.stack([shared_out[i][k] for i in range(layers)]) for k in range(4)]
    return (
        result_out, grad_out, shared[0], heads[0], heads[1], shared[1], heads[2], heads[3],
        shared[2], shared[3], heads[4], heads[5], heads[6], heads[7], heads[8],
    )


def solution(mesh):
    placed = (
        P(("dp", "row"), None),
        P("dp", None),
        P(("dp", "row"), None),
        P(),
        P(None, "col", "row"),
        P(None, "col", "row"),
        P(),
        P(None, None, ("row", "col")),
        P(None, ("row", "col")),
        P(),
        P(),
        P(None, ("row", "col")),
        P(None, ("row", "col")),
        P(None, ("row", "col")),
        P(None, ("row", "col")),
        P(None, ("row", "col"), None),
    )
    return jax.shard_map(
        shards,
        mesh=mesh,
        in_specs=placed,
        out_specs=(
            P(("dp", "row"), None),
            P(("dp", "row"), None),
            P(),
            P(None, "col", "row"),
            P(None, "col", "row"),
            P(),
            P(None, None, ("row", "col")),
            P(None, ("row", "col")),
            P(),
            P(),
            P(None, ("row", "col")),
            P(None, ("row", "col")),
            P(None, ("row", "col")),
            P(None, ("row", "col")),
            P(None, ("row", "col"), None),
        ),
        check_vma=False,
    )
```

```python
import jax
import jax.numpy as jnp
from jax import lax
from jax.experimental import pallas as pl
from jax.experimental.pallas import tpu as pltpu
from jax.sharding import PartitionSpec as P

EPS = 1e-05
BF = jnp.bfloat16
F32 = jnp.float32
HEAD_DIM = 64
STATE = 128
LANES = 128
NN = (((1,), (0,)), ((), ()))
NT = (((1,), (1,)), ((), ()))
TN = (((0,), (0,)), ((), ()))
VMEM_BYTES = 58 * 1024 * 1024


def dot(left, right, dims=NN):
    return lax.dot_general(left, right, dims, preferred_element_type=F32)


def shape(dims, dtype):
    return jax.ShapeDtypeStruct(dims, dtype)


def local_call(body, outs, scalars, arrays, scratch=(), name=None):
    smem = pl.BlockSpec(memory_space=pltpu.SMEM)
    vmem = pl.BlockSpec(memory_space=pltpu.VMEM)
    return pl.pallas_call(
        body,
        out_shape=tuple(outs),
        in_specs=[smem] * len(scalars) + [vmem] * len(arrays),
        out_specs=tuple(vmem for _ in outs),
        scratch_shapes=list(scratch),
        compiler_params=pltpu.CompilerParams(vmem_limit_bytes=VMEM_BYTES),
        name=name,
    )(*scalars, *arrays)


def ring_dest(index, step):
    return lax.rem(index + step, 4)


def ring_source(index, step):
    return lax.rem(index + 4 - step, 4)


def peer(index, step):
    return index ^ step


def block(index, size):
    return pl.ds(pl.multiple_of(index * size, size), size)


def across_heads(pieces):
    return [pieces[0]] + [
        lax.ppermute(pieces[step], "col", [(i, (i + step) % 4) for i in range(4)])
        for step in range(1, 4)
    ]


def across_tokens(pieces):
    return [pieces[0]] + [
        lax.ppermute(pieces[step], "row", [(i, i ^ step) for i in range(4)]) for step in range(1, 4)
    ]


def transposed(array):
    return lax.ppermute(
        array, ("row", "col"), [(i * 4 + j, j * 4 + i) for i in range(4) for j in range(4)]
    )


def added(pieces):
    total = pieces[0].astype(F32)
    for piece in pieces[1:]:
        total = total + piece.astype(F32)
    return total.astype(BF)


def parity_sum(array):
    count = lax.axis_size("dp")
    moved = [
        lax.ppermute(array, "dp", [(i, (i + step) % count) for i in range(count)])
        for step in range(2, count, 2)
    ]
    return added([array, *moved]) if moved else array


def pair_swap(array):
    count = lax.axis_size("dp")
    return lax.ppermute(array, "dp", [(i, i ^ 1) for i in range(count)])


def copies_sum(array):
    if lax.axis_size("dp") > 2:
        return lax.psum(array, "dp").astype(F32)
    return array.astype(F32) + pair_swap(array).astype(F32)


def split_wide(value, rows):
    high = value.astype(BF).astype(F32)
    lane = lax.broadcasted_iota(jnp.int32, (rows, LANES), 1)
    return jnp.where(lane < 64, high, value - high)


def join_wide(lanes):
    return lanes[:, 0:1] + lanes[:, 64:65]


def start_body(tokens_ref, gain_ref, resid_ref, normed_ref, scale_ref):
    resid = tokens_ref[...].astype(F32)
    width = resid.shape[1]
    scale = lax.rsqrt(jnp.sum(resid * resid, axis=1, keepdims=True) / width + EPS)
    resid_ref[...] = resid
    normed_ref[...] = (resid * scale * gain_ref[...]).astype(BF)
    scale_ref[...] = jnp.broadcast_to(scale, scale_ref.shape)


def collect_branch(own_ref, others, inner):
    total = own_ref[...]
    for other in others:
        total = total + other[...].astype(F32)
    width = total.shape[1] - LANES
    inverse = lax.rsqrt(join_wide(total[:, width:]) / inner + EPS)
    return total[:, :width], inverse


def middle_body(inner, own, one, two, three, resid_ref, gain_ref, next_ref, mixed_ref, inv_ref,
                normed_ref, scale_ref):
    mixed, inverse = collect_branch(own, (one, two, three), inner)
    resid = resid_ref[...] + inverse * mixed
    width = resid.shape[1]
    scale = lax.rsqrt(jnp.sum(resid * resid, axis=1, keepdims=True) / width + EPS)
    next_ref[...] = resid
    mixed_ref[...] = mixed
    inv_ref[...] = jnp.broadcast_to(inverse, inv_ref.shape)
    normed_ref[...] = (resid * scale * gain_ref[...]).astype(BF)
    scale_ref[...] = jnp.broadcast_to(scale, scale_ref.shape)


def send_grad(grad, mixed, inverse, inner, out_ref):
    rows, width = grad.shape
    scaled = (grad * inverse).astype(BF)
    along = jnp.sum(scaled.astype(F32) * mixed, axis=1, keepdims=True)
    factor = inverse * inverse * along / inner
    out_ref[:, :width] = scaled
    out_ref[:, width:] = split_wide(factor, rows).astype(BF)


def turn_body(inner, own, one, two, three, resid_ref, cot_ref, result_ref, sent_ref):
    mixed, inverse = collect_branch(own, (one, two, three), inner)
    result_ref[...] = (resid_ref[...] + inverse * mixed).astype(BF)
    send_grad(cot_ref[...].astype(F32), mixed, inverse, inner, sent_ref)


def norm_back(own, others, grad, resid, scale, gain):
    total = own[...]
    for other in others:
        total = total + other[...].astype(F32)
    weighted = total * gain
    width = resid.shape[1]
    along = jnp.sum(resid * weighted, axis=1, keepdims=True)
    return grad + scale * weighted - resid * (scale * scale * scale * along / width)


def back_middle_body(inner, own, one, two, three, grad_ref, resid_ref, scale_ref, gain_ref,
                     mixed_ref, inv_ref, out_ref, sent_ref):
    grad = norm_back(own, (one, two, three), grad_ref[...].astype(F32), resid_ref[...],
                     scale_ref[:, 0:1], gain_ref[...])
    out_ref[...] = grad
    send_grad(grad, mixed_ref[...], inv_ref[:, 0:1], inner, sent_ref)


def back_end_body(own, one, two, three, grad_ref, resid_ref, scale_ref, gain_ref, out_ref):
    grad = norm_back(own, (one, two, three), grad_ref[...], resid_ref[...], scale_ref[:, 0:1],
                     gain_ref[...])
    out_ref[...] = grad.astype(BF)


def place_body(place_ref, a0, a1, a2, a3, b0, b1, b2, b3, low_ref, wide_ref):
    row = place_ref[0]
    for step, (low, wide) in enumerate(((a0, b0), (a1, b1), (a2, b2), (a3, b3))):
        rows = block(ring_source(row, step), low.shape[0])
        low_ref[rows, :] = low[...]
        wide_ref[rows, :] = wide[...].astype(F32)


def tied(first, second):
    both = lax.optimization_barrier((tuple(first), tuple(second)))
    return list(both[0]), list(both[1])


def joined_weights(place_ref, weights, mine_s, other_s):
    if len(weights) == 2:
        return weights
    for step in range(4):
        rows = block(peer(place_ref[1], step), 128)
        mine_s[rows, :] = weights[step][...]
        other_s[rows, :] = weights[4 + step][...]
    return mine_s, other_s


def project_in_body(place_ref, x0, x1, x2, x3, *refs):
    *weights, side_ref, normed_ref, m0, m1, m2, m3, mine_s, other_s = refs
    row, col, half = place_ref[0], place_ref[1], place_ref[2]
    mine_ref, other_ref = joined_weights(place_ref, weights, mine_s, other_s)
    for step, piece in enumerate((x0, x1, x2, x3)):
        normed_ref[block(ring_source(row, step), 64), :] = piece[...]
    mine = jnp.concatenate([normed_ref[:, block(2 * j + half, 128)] for j in range(4)], axis=1)
    other = jnp.concatenate([normed_ref[:, block(2 * j + 1 - half, 128)] for j in range(4)], axis=1)
    side = dot(normed_ref[...], side_ref[...]).astype(BF)
    width = mine_ref.shape[1] - LANES
    steps = dot(mine, mine_ref[:, width:]) + dot(other, other_ref[:, width:])
    steps = steps.astype(BF).astype(F32).T[0:16, :].astype(BF)
    for step, out in enumerate((m0, m1, m2, m3)):
        cols = block(peer(col, step), 256)
        value = dot(mine, mine_ref[:, cols]) + dot(other, other_ref[:, cols])
        out[0:256, 0:256] = value.astype(BF)
        out[0:256, 256:512] = side
        out[256:272, 0:256] = steps
        out[256:272, 256:512] = jnp.zeros((16, 256), BF)


def sigmoid(value):
    return 1.0 / (1.0 + jnp.exp(-value))


def lane_scan(value):
    length = value.shape[1]
    lane = lax.broadcasted_iota(jnp.int32, value.shape, 1)
    step = 1
    while step < length:
        value = value + jnp.where(lane >= step, pltpu.roll(value, step, 1), 0.0)
        step *= 2
    return value


def lane_scan_back(value):
    length = value.shape[1]
    lane = lax.broadcasted_iota(jnp.int32, value.shape, 1)
    step = 1
    while step < length:
        value = value + jnp.where(
            lane < length - step, pltpu.roll(value, length - step, 1), 0.0
        )
        step *= 2
    return value


def gather_sequence(col, pieces, zx_s, bc_s, dt_s):
    for step, piece in enumerate(pieces):
        at = peer(col, step)
        zx_s[block(at, 256), :] = piece[0:256, 0:256]
        bc_s[block(at, 256), :] = piece[0:256, 256:512]
        dt_s[:, block(at, 256)] = piece[256:272, 0:256].astype(F32)


def step_rows(col, dt_s, params):
    raw = dt_s[...]
    at = lax.broadcasted_iota(jnp.int32, raw.shape, 0)
    first = jnp.sum(jnp.where(at == 2 * col, raw, 0.0), axis=0, keepdims=True) + params[0]
    second = jnp.sum(jnp.where(at == 2 * col + 1, raw, 0.0), axis=0, keepdims=True) + params[1]
    at8 = lax.broadcasted_iota(jnp.int32, (8, raw.shape[1]), 0)
    pre = jnp.where(at8 == 0, first, second)
    steps = jnp.maximum(pre, 0.0) + jnp.log1p(jnp.exp(-jnp.abs(pre)))
    rate = jnp.where(at8 == 0, params[2], params[3])
    return pre, steps, rate, lane_scan(steps * rate)


def conv_pre(values, taps, masks_ref):
    total = taps[4:5, :] + taps[0:1, :] * values
    for offset in range(1, 4):
        moved = pltpu.roll(values, offset, 0) * masks_ref[:, offset:offset + 1]
        total = total + taps[offset:offset + 1, :] * moved
    return total


def head_pre(head, zx_s, taps_ref, masks_ref):
    values = zx_s[:, head * 128:head * 128 + 128].astype(F32)
    lane = lax.broadcasted_iota(jnp.int32, values.shape, 1)
    conv = conv_pre(values, taps_ref[head * 8:head * 8 + 8, :], masks_ref)
    return values, jnp.where(lane < 64, values, conv)


def reach(i, j, masks_ref, seg_ref):
    same = masks_ref[i * 256:i * 256 + 256, 0:1] == seg_ref[0:1, j * 256:j * 256 + 256]
    if i == j:
        at = lax.broadcasted_iota(jnp.int32, (256, 256), 0)
        to = lax.broadcasted_iota(jnp.int32, (256, 256), 1)
        same = same & (at >= to)
    return same


def pairs():
    return [(i, j) for i in range(4) for j in range(max(0, i - 2), i + 1)]


def mix_body(place_ref, params, m0, m1, m2, m3, masks_ref, seg_ref, taps_ref, side_taps_ref,
             y_ref, g0, g1, g2, g3, zx_s, bc_s, dt_s, src_s, src_low, b_s, c_s, row_s, col_s, acc_s,
             g_s):
    col = place_ref[1]
    gather_sequence(col, (m0, m1, m2, m3), zx_s, bc_s, dt_s)
    pre, steps, rate, cum = step_rows(col, dt_s, params)
    row_s[0:8, :] = steps
    row_s[8:16, :] = cum
    col_s[...] = jnp.concatenate([cum, jnp.zeros((120, cum.shape[1]), F32)], axis=0).T
    for head in range(2):
        values, active = head_pre(head, zx_s, taps_ref, masks_ref)
        active = active * sigmoid(active)
        src_s[:, head * 128:head * 128 + 128] = active
        src_low[:, head * 128:head * 128 + 128] = active.astype(BF)
    for part, out in enumerate((b_s, c_s)):
        lanes = slice(part * 128, part * 128 + 128)
        conv = conv_pre(bc_s[:, lanes].astype(F32), side_taps_ref[:, lanes], masks_ref)
        out[...] = (conv * sigmoid(conv)).astype(BF)
    acc_s[...] = jnp.zeros_like(acc_s)
    for i, j in pairs():
        ri, rj = slice(i * 256, i * 256 + 256), slice(j * 256, j * 256 + 256)
        affinity = dot(c_s[ri, :], b_s[rj, :], NT)
        allowed = reach(i, j, masks_ref, seg_ref)
        for head in range(2):
            lanes = slice(head * 128, head * 128 + 128)
            span = col_s[ri, head:head + 1] - row_s[8 + head:9 + head, rj]
            weight = jnp.exp(jnp.where(allowed, span, -1e30)) * affinity * row_s[head:head + 1, rj]
            acc_s[ri, lanes] += dot(weight.astype(BF), src_low[rj, lanes])
    lane = lax.broadcasted_iota(jnp.int32, (1024, 128), 1)
    y0 = acc_s[:, 0:128] + params[4] * src_s[:, 0:128]
    y1 = acc_s[:, 128:256] + params[5] * src_s[:, 128:256]
    y = jnp.where(lane < 64, pltpu.roll(y0, 64, 1), y1)
    gate = jnp.where(lane < 64, src_s[:, 0:128], pltpu.roll(src_s[:, 128:256], 64, 1))
    y_ref[...] = y
    g_s[...] = (y * gate).astype(BF)
    for step, out in enumerate((g0, g1, g2, g3)):
        out[...] = g_s[block(peer(col, step), 256), :]


def mix_back_body(place_ref, params, d0, d1, d2, d3, m0, m1, m2, m3, y_ref, masks_ref, seg_ref,
                  taps_ref, side_taps_ref, o0, o1, o2, o3, head_ref, side_ref, small_ref,
                  zx_s, bc_s, dt_s, src_s, src_low, slope_s, bc_low, bc_slope, row_s, col_s,
                  dy_s, dy_low, dgy_s, dsrc_s, dbc_s, rows_s, cols_s, dg_s, out_zx, out_bc, out_dt):
    col = place_ref[1]
    gather_sequence(col, (m0, m1, m2, m3), zx_s, bc_s, dt_s)
    for step, piece in enumerate((d0, d1, d2, d3)):
        dg_s[block(peer(col, step), 256), :] = piece[...].astype(F32)
    pre, steps, rate, cum = step_rows(col, dt_s, params)
    row_s[0:8, :] = steps
    row_s[8:16, :] = cum
    col_s[...] = jnp.concatenate([cum, jnp.zeros((120, cum.shape[1]), F32)], axis=0).T
    lane = lax.broadcasted_iota(jnp.int32, (1024, 128), 1)
    skips = []
    for head in range(2):
        lanes = slice(head * 128, head * 128 + 128)
        values, active = head_pre(head, zx_s, taps_ref, masks_ref)
        sig = sigmoid(active)
        source = active * sig
        slope = sig * (1.0 + active * (1.0 - sig))
        src_low[:, lanes] = source.astype(BF)
        slope_s[:, lanes] = slope
        grad = dg_s[...] if head == 0 else pltpu.roll(dg_s[...], 64, 1)
        y = y_ref[...] if head == 0 else pltpu.roll(y_ref[...], 64, 1)
        dgy_s[:, lanes] = grad * y * slope
        dy = jnp.where(lane < 64, 0.0, pltpu.roll(grad * source, 64, 1))
        dy_low[:, lanes] = dy.astype(BF)
        dsrc_s[:, lanes] = params[4 + head] * dy
        skips.append(jnp.sum(dy * source))
    for part in range(2):
        lanes = slice(part * 128, part * 128 + 128)
        conv = conv_pre(bc_s[:, lanes].astype(F32), side_taps_ref[:, lanes], masks_ref)
        sig = sigmoid(conv)
        bc_low[:, lanes] = (conv * sig).astype(BF)
        bc_slope[:, lanes] = sig * (1.0 + conv * (1.0 - sig))
    dbc_s[...] = jnp.zeros_like(dbc_s)
    rows_s[...] = jnp.zeros_like(rows_s)
    cols_s[...] = jnp.zeros_like(cols_s)
    lane256 = lax.broadcasted_iota(jnp.int32, (256, 128), 1)
    for i, j in pairs():
        ri, rj = slice(i * 256, i * 256 + 256), slice(j * 256, j * 256 + 256)
        affinity = dot(bc_low[ri, 128:256], bc_low[rj, 0:128], NT)
        allowed = reach(i, j, masks_ref, seg_ref)
        shared = None
        for head in range(2):
            lanes = slice(head * 128, head * 128 + 128)
            span = col_s[ri, head:head + 1] - row_s[8 + head:9 + head, rj]
            decay = jnp.exp(jnp.where(allowed, span, -1e30))
            step = row_s[head:head + 1, rj]
            inner = dot(dy_low[ri, lanes], src_low[rj, lanes], NT)
            weight = (decay * affinity * step).astype(BF)
            dsrc_s[rj, lanes] += dot(weight, dy_low[ri, lanes], TN)
            both = decay * inner
            term = both * step
            shared = term if shared is None else shared + term
            product = affinity * both
            cols_s[head:head + 1, rj] += jnp.sum(product, axis=0, keepdims=True)
            total = jnp.sum(affinity * term, axis=1, keepdims=True)
            rows_s[ri, :] += jnp.where(lane256 == head, total, 0.0)
        low = shared.astype(BF)
        dbc_s[ri, 128:256] += dot(low, bc_low[rj, 0:128])
        dbc_s[rj, 0:128] += dot(low, bc_low[ri, 128:256], TN)
    sums = rows_s[...].T[0:8, :]
    col_sum = cols_s[...]
    back = lane_scan_back(sums - col_sum * steps)
    dstep = col_sum + rate * back
    at8 = lax.broadcasted_iota(jnp.int32, steps.shape, 0)
    dlog = rate * jnp.sum(steps * back, axis=1, keepdims=True)
    draw = dstep * sigmoid(pre)
    dbias = jnp.sum(draw, axis=1, keepdims=True)
    lane8 = lax.broadcasted_iota(jnp.int32, (8, 128), 1)
    row8 = lax.broadcasted_iota(jnp.int32, (8, 128), 0)
    dskip = jnp.where(row8 == 0, skips[0], skips[1])
    small_ref[...] = jnp.where(
        lane8 == 0, dbias, jnp.where(lane8 == 1, dlog[:, 0:1], jnp.where(lane8 == 2, dskip, 0.0))
    )
    at16 = lax.broadcasted_iota(jnp.int32, (16, 1024), 0)
    out_dt[...] = jnp.where(
        at16 == 2 * col, draw[0:1, :], jnp.where(at16 == 2 * col + 1, draw[1:2, :], 0.0)
    ).astype(BF)

    def conv_back(values, du, taps, out_ref, rows, lanes):
        dv = taps[0:1, :] * du
        out_ref[rows:rows + 1, lanes] = jnp.sum(du * values, axis=0, keepdims=True)
        for offset in range(1, 4):
            masked = du * masks_ref[:, offset:offset + 1]
            out_ref[rows + offset:rows + offset + 1, lanes] = jnp.sum(
                masked * pltpu.roll(values, offset, 0), axis=0, keepdims=True
            )
            dv = dv + taps[offset:offset + 1, :] * pltpu.roll(masked, 1024 - offset, 0)
        out_ref[rows + 4:rows + 5, lanes] = jnp.sum(du, axis=0, keepdims=True)
        return dv

    head_ref[...] = jnp.zeros_like(head_ref)
    side_ref[...] = jnp.zeros_like(side_ref)
    for head in range(2):
        lanes = slice(head * 128, head * 128 + 128)
        values = zx_s[:, lanes].astype(F32)
        du = jnp.where(lane < 64, 0.0, dsrc_s[:, lanes] * slope_s[:, lanes])
        taps = taps_ref[head * 8:head * 8 + 8, :]
        dv = conv_back(values, du, taps, head_ref, head * 8, slice(0, 128))
        out_zx[:, lanes] = jnp.where(lane < 64, dgy_s[:, lanes], dv).astype(BF)
    for part in range(2):
        lanes = slice(part * 128, part * 128 + 128)
        values = bc_s[:, lanes].astype(F32)
        du = dbc_s[:, lanes] * bc_slope[:, lanes]
        dv = conv_back(values, du, side_taps_ref[:, lanes], side_ref, 0, lanes)
        out_bc[:, lanes] = dv.astype(BF)
    for step, out in enumerate((o0, o1, o2, o3)):
        at = peer(col, step)
        out[0:256, 0:256] = out_zx[block(at, 256), :]
        out[0:256, 256:512] = out_bc[block(at, 256), :]
        out[256:272, 0:256] = out_dt[:, block(at, 256)]
        out[256:272, 256:512] = jnp.zeros((16, 256), BF)


def project_out_body(place_ref, g0, g1, g2, g3, *refs):
    *weights, full_ref, o0, o1, o2, o3, acc_s, mine_s, other_s = refs
    row, col, half = place_ref[0], place_ref[1], place_ref[2]
    mine_ref, other_ref = joined_weights(place_ref, weights, mine_s, other_s)
    for step, piece in enumerate((g0, g1, g2, g3)):
        full_ref[:, block(peer(col, step), 128)] = piece[...]
    full = full_ref[...]
    width = 2 * mine_ref.shape[1]
    acc_s[:, block(half, width // 2)] = dot(full, mine_ref[...])
    acc_s[:, block(1 - half, width // 2)] = dot(full, other_ref[...])
    wide = full.astype(F32)
    acc_s[:, width:] = split_wide(jnp.sum(wide * wide, axis=1, keepdims=True), wide.shape[0])
    for step, out in enumerate((o0, o1, o2, o3)):
        out[...] = acc_s[block(ring_dest(row, step), 64), :].astype(out.dtype)


def out_back_body(place_ref, q0, q1, q2, q3, *refs):
    *weights, full_ref, grad_ref, gain_ref, d0, d1, d2, d3, dg_s, fac_s, mine_s, other_s = refs
    row, col, half = place_ref[0], place_ref[1], place_ref[2]
    mine_ref, other_ref = joined_weights(place_ref, weights, mine_s, other_s)
    width = grad_ref.shape[1]
    for step, piece in enumerate((q0, q1, q2, q3)):
        rows = block(ring_source(row, step), 64)
        grad_ref[rows, :] = piece[:, 0:width]
        fac_s[rows, :] = piece[:, width:].astype(F32)
    value = dot(grad_ref[:, block(half, width // 2)], mine_ref[...], NT)
    value = value + dot(grad_ref[:, block(1 - half, width // 2)], other_ref[...], NT)
    full = full_ref[...].astype(F32)
    gain_ref[...] = (value * full).astype(BF)
    dg_s[...] = (value - full * join_wide(fac_s[...])).astype(BF)
    for step, out in enumerate((d0, d1, d2, d3)):
        out[...] = dg_s[:, block(peer(col, step), 128)]


def out_weight_body(place_ref, full_ref, grad_ref, gain_ref, keep_ref, give_ref, acc_s):
    col, half = place_ref[1], place_ref[2]
    width = grad_ref.shape[1]
    acc_s[:, 0:width] = dot(full_ref[...], grad_ref[...], TN).astype(BF)
    ones = jnp.ones((gain_ref.shape[0], LANES), BF)
    acc_s[:, width:] = dot(gain_ref[...], ones, TN).astype(BF)
    for step in range(4):
        at = 2 * peer(col, step)
        keep_ref[step * 64:step * 64 + 64, :] = acc_s[block(at + half, 64), :]
        give_ref[step * 64:step * 64 + 64, :] = acc_s[block(at + 1 - half, 64), :]


def in_back_body(place_ref, d0, d1, d2, d3, *refs):
    *weights, side_ref, normed_ref, full_ref, dside_ref, gain_ref, o0, o1, o2, o3 = refs[:-3]
    dx_s, mine_s, other_s = refs[-3:]
    row, col, half = place_ref[0], place_ref[1], place_ref[2]
    mine_ref, other_ref = joined_weights(place_ref, weights, mine_s, other_s)
    pieces = (d0, d1, d2, d3)
    side = None
    steps = None
    for step, piece in enumerate(pieces):
        full_ref[:, block(peer(col, step), 256)] = piece[0:256, 0:256]
        part = piece[0:256, 256:512].astype(F32)
        more = piece[256:272, 0:256].astype(F32)
        side = part if side is None else side + part
        steps = more if steps is None else steps + more
    dside = side.astype(BF)
    dside_ref[...] = dside
    width = full_ref.shape[1] - LANES
    full_ref[:, width:] = jnp.concatenate([steps, jnp.zeros((112, 256), F32)], axis=0).T.astype(BF)
    full = full_ref[...]
    mine = dot(full, mine_ref[...], NT)
    other = dot(full, other_ref[...], NT)
    for j in range(4):
        dx_s[:, block(2 * j + half, 128)] = mine[:, j * 128:j * 128 + 128]
        dx_s[:, block(2 * j + 1 - half, 128)] = other[:, j * 128:j * 128 + 128]
    dx_s[...] += dot(dside, side_ref[...], NT)
    gains = jnp.sum(dx_s[...] * normed_ref[...].astype(F32), axis=0, keepdims=True)
    gain_ref[...] = jnp.broadcast_to(gains, gain_ref.shape)
    for step, out in enumerate((o0, o1, o2, o3)):
        out[...] = dx_s[block(ring_dest(row, step), 64), :].astype(out.dtype)


def in_weight_body(place_ref, normed_ref, full_ref, dside_ref, gains_ref, gain_ref, taps_ref,
                   keep_ref, give_ref, keep_side, give_side, acc_s, side_s):
    col, half = place_ref[1], place_ref[2]
    normed = normed_ref[...]
    width = normed.shape[1]
    acc_s[...] = dot(normed, full_ref[...], TN).astype(BF)
    side_s[0:width, :] = dot(normed, dside_ref[...], TN).astype(BF)
    gains = gains_ref[0:1, :] / gain_ref[...]
    rows = [gains[:, at * 256:at * 256 + 256] for at in range(width // 256)]
    rows.append(taps_ref[0:5, :])
    rows.append(jnp.zeros((123 - width // 256, 256), F32))
    side_s[width:, :] = jnp.concatenate(rows, axis=0).astype(BF)
    for step in range(4):
        at = 2 * peer(col, step)
        keep_ref[step * 128:step * 128 + 128, :] = acc_s[block(at + half, 128), :]
        give_ref[step * 128:step * 128 + 128, :] = acc_s[block(at + 1 - half, 128), :]
    size = keep_side.shape[0]
    keep_side[...] = side_s[block(half, size), :]
    give_side[...] = side_s[block(1 - half, size), :]


def combine_body(count, *refs):
    pairs_in, outs = refs[:2 * count], refs[2 * count:]
    for step, out in enumerate(outs):
        base = 0
        for index in range(count):
            keep, got = pairs_in[2 * index], pairs_in[2 * index + 1]
            size = keep.shape[0] // 4
            rows = slice(step * size, step * size + size)
            total = keep[rows, :].astype(F32) + got[rows, :].astype(F32)
            out[base:base + size, :] = total.astype(out.dtype)
            base += size


def combine_side_body(place_ref, keep, got, o0, o1, o2, o3, acc_s):
    acc_s[...] = (keep[...].astype(F32) + got[...].astype(F32)).astype(BF)
    for step, out in enumerate((o0, o1, o2, o3)):
        out[...] = acc_s[block(peer(place_ref[1], step), out.shape[0]), :]


def quarters_body(place_ref, a0, a1, a2, a3, out_ref):
    for step, piece in enumerate((a0, a1, a2, a3)):
        out_ref[block(peer(place_ref[1], step), piece.shape[0]), :] = piece[...]


def finish_body(layers, place_ref, *refs):
    sides, grads, gain_ref = refs[:2 * layers], refs[2 * layers:4 * layers], refs[4 * layers]
    zx_ref, dt_ref, out_ref, gain_out, side_ref, rest_ref, side_s = refs[4 * layers + 1:]
    half = place_ref[2]
    for layer in range(layers):
        mine, other = sides[2 * layer], sides[2 * layer + 1]
        size = mine.shape[0]
        side_s[block(half, size), :] = mine[...].astype(F32)
        side_s[block(1 - half, size), :] = other[...].astype(F32)
        rows = side_ref.shape[1]
        side_ref[layer] = side_s[0:rows, :]
        rest_ref[layer] = side_s[rows:, :]
    width = zx_ref.shape[2]
    for layer in range(layers):
        at = 2 * (layers - 1 - layer)
        group = grads[at:at + 2]
        for part, which in zip(group, (half, 1 - half)):
            rows = block(which, 128)
            zx_ref[layer, rows, :] = part[0:128, 0:width].astype(F32)
            dt_ref[layer, rows, :] = part[0:128, width:].astype(F32)
            rows = block(which, 64)
            gain = gain_ref[layer, rows, :]
            out_ref[layer, rows, :] = part[128:192, 0:width].astype(F32) * gain[:, 0:1]
            gain_out[layer, rows, :] = part[128:192, width:].astype(F32) / gain


def shards(
    hidden,
    segments,
    cotangent,
    norm_gain,
    zx_weight,
    dt_weight,
    bc_weight,
    conv_x,
    conv_x_bias,
    conv_bc,
    conv_bc_bias,
    dt_bias,
    a_log,
    skip_d,
    gnorm_gain,
    out_weight,
):
    row, col, copy = lax.axis_index("row"), lax.axis_index("col"), lax.axis_index("dp")
    half = copy % 2
    layers, width = norm_gain.shape
    length = segments.shape[1]
    heads_here = dt_weight.shape[2]
    inner = 4 * 4 * conv_x.shape[2]
    place = jnp.stack([col, row, half, row]).astype(jnp.int32)

    tokens = lax.dynamic_slice_in_dim(hidden, col * 64, 64, 0)
    cot = lax.dynamic_slice_in_dim(cotangent, col * 64, 64, 0)

    def half_in(layer):
        mine = lax.dynamic_slice_in_dim(zx_weight[layer], half * 128, 128, 0)
        steps = lax.dynamic_slice_in_dim(dt_weight[layer], half * 128, 128, 0)
        return jnp.concatenate(
            [mine, jnp.pad(steps, ((0, 0), (0, LANES - heads_here)))], axis=1
        )

    def half_out(layer):
        mine = lax.dynamic_slice_in_dim(out_weight[layer], half * (width // 2), width // 2, 1)
        return (gnorm_gain[layer][:, None] * mine.astype(F32)).astype(BF)

    def spread(array):
        pieces = across_tokens([transposed(array)] * 4)
        return pieces, [pair_swap(piece) for piece in pieces]

    in_mine, in_other = spread(half_in(0))
    in_mine, (out_half,) = tied(in_mine, [half_out(0)])
    out_mine, out_other = spread(out_half)
    rest = []
    for layer in range(1, layers):
        rest += [half_in(layer), half_out(layer)]
    sizes = [piece.shape[1] for piece in rest]
    out_mine, (rest,) = tied(out_mine, [jnp.concatenate(rest, axis=1)])
    rest = lax.all_gather(transposed(rest), "row", axis=0, tiled=True)
    in_weights = [[*in_mine, *in_other]]
    out_weights = [[*out_mine, *out_other]]
    cuts = [sum(sizes[:at]) for at in range(len(sizes) + 1)]
    out_scratch = [pltpu.VMEM((512, width // 2), BF)] * 2

    packed = jnp.concatenate(
        [
            conv_x,
            conv_x_bias[:, None],
            jnp.pad(
                jnp.concatenate([dt_bias, -jnp.exp(a_log), skip_d], axis=1),
                ((0, 0), (0, LANES - 6)),
            )[:, None],
            jnp.zeros((layers, 2, LANES), F32),
        ],
        axis=1,
    )
    packed = transposed(packed)

    seg = segments[0].astype(F32)
    columns = [seg]
    for offset in range(1, 4):
        earlier = jnp.concatenate([jnp.full((offset,), -1.0, F32), seg[:-offset]])
        columns.append((earlier == seg).astype(F32))
    masks = jnp.pad(jnp.stack(columns, axis=1), ((0, 0), (0, LANES - 4)))
    seg_rows = jnp.broadcast_to(seg[None], (8, length))
    taps_x = packed[:, :5].reshape(layers, 5, 2, 64)
    taps_x = jnp.pad(taps_x.transpose(0, 2, 1, 3), ((0, 0), (0, 0), (0, 3), (64, 0)))
    taps_x = taps_x.reshape(layers, 16, LANES)
    taps_bc = jnp.pad(
        jnp.concatenate([conv_bc, conv_bc_bias[:, None]], axis=1), ((0, 0), (0, 3), (0, 0))
    )
    params = packed[:, 5, :8]
    gains = norm_gain[:, None]

    wide = width + LANES
    kept = []
    resid, normed, scale = local_call(
        start_body,
        [shape((64, width), F32), shape((64, width), BF), shape((64, LANES), F32)],
        [], [tokens, gains[0]], name="start",
    )
    for layer in range(layers):
        pieces = across_heads([normed] * 4)
        full_normed, *sent = local_call(
            project_in_body,
            [shape((256, width), BF)] + [shape((272, 512), BF)] * 4,
            [place], [*pieces, *in_weights[layer], bc_weight[layer]],
            [pltpu.VMEM((512, wide), BF)] * 2, name="project_in",
        )
        mixed_in = across_tokens(sent)
        y, *sent = local_call(
            mix_body,
            [shape((length, 128), F32)] + [shape((256, 128), BF)] * 4,
            [place, params[layer]],
            [*mixed_in, masks, seg_rows, taps_x[layer], taps_bc[layer]],
            [
                pltpu.VMEM((length, 256), BF),
                pltpu.VMEM((length, 256), BF),
                pltpu.VMEM((16, length), F32),
                pltpu.VMEM((length, 256), F32),
                pltpu.VMEM((length, 256), BF),
                pltpu.VMEM((length, 128), BF),
                pltpu.VMEM((length, 128), BF),
                pltpu.VMEM((16, length), F32),
                pltpu.VMEM((length, 128), F32),
                pltpu.VMEM((length, 256), F32),
                pltpu.VMEM((length, 128), BF),
            ],
            name="mix",
        )
        gated = across_tokens(sent)
        full_gated, *sent = local_call(
            project_out_body,
            [shape((256, 512), BF), shape((64, wide), F32)] + [shape((64, wide), BF)] * 3,
            [place], [*gated, *out_weights[layer]],
            [pltpu.VMEM((256, wide), F32)] + out_scratch, name="project_out",
        )
        parts = across_heads(sent)
        if layer == 0:
            parts, (rest,) = tied(parts, [rest])
            other = pair_swap(rest)
            both = [
                [whole[:, cuts[at]:cuts[at + 1]] for whole in (rest, other)]
                for at in range(len(sizes))
            ]
            in_weights += both[0::2]
            out_weights += both[1::2]
        entry = [resid, scale, full_normed, mixed_in, y, full_gated]
        if layer + 1 < layers:
            resid, mixed, inverse, normed, scale = local_call(
                lambda *refs: middle_body(inner, *refs),
                [shape((64, width), F32), shape((64, width), F32), shape((64, LANES), F32),
                 shape((64, width), BF), shape((64, LANES), F32)],
                [], [*parts, resid, gains[layer + 1]], name="middle",
            )
            entry += [mixed, inverse]
        else:
            result, sent_grad = local_call(
                lambda *refs: turn_body(inner, *refs),
                [shape((64, width), BF), shape((64, wide), BF)],
                [], [*parts, resid, cot], name="turn",
            )
        kept.append(entry)

    grad = cot
    smalls, sides, grads = [None] * layers, [None] * layers, [None] * layers
    arrived = [None] * layers

    def side_messages(terms):
        side = local_call(
            combine_side_body, [shape((144, 256), BF)] * 4, [place], terms[:2],
            [pltpu.VMEM((576, 256), BF)], name="combine_side",
        )
        sent = local_call(
            lambda *refs: combine_body(2, *refs),
            [shape((192, wide), F32)] + [shape((192, wide), BF)] * 3, [], terms[2:],
            name="combine",
        )
        return [*side, *sent]

    home, waiting = None, []
    for layer in reversed(range(layers)):
        resid, scale, full_normed, mixed_in, y, full_gated = kept[layer][:6]
        pieces = across_heads([sent_grad] * 4)
        if waiting:
            pieces, waiting = tied(pieces, side_messages(waiting))
        full_grad, gain_terms, *sent = local_call(
            out_back_body,
            [shape((256, width), BF), shape((256, 512), BF)] + [shape((256, 128), BF)] * 4,
            [place], [*pieces, *out_weights[layer], full_gated],
            [pltpu.VMEM((256, 512), BF), pltpu.VMEM((256, LANES), F32)] + out_scratch,
            name="out_back",
        )
        dgated = across_tokens(sent)
        keep, give = local_call(
            out_weight_body, [shape((256, wide), BF)] * 2, [place],
            [full_gated, full_grad, gain_terms], [pltpu.VMEM((512, wide), BF)], name="out_weight",
        )
        dgated, (keep_out, give_out) = tied(dgated, [keep, give])
        if home is None:
            dgated, (result,) = tied(dgated, [result])
            home = across_heads([result] * 4)
        if waiting:
            dgated, waiting = tied(dgated, waiting)
            waiting = [*across_tokens(waiting[:4]), *across_tokens(waiting[4:])]
        o0, o1, o2, o3, head_grads, side_grads, small_grads = local_call(
            mix_back_body,
            [shape((272, 512), BF)] * 4
            + [shape((16, LANES), F32), shape((8, 256), F32), shape((8, LANES), F32)],
            [place, params[layer]],
            [*dgated, *mixed_in, y, masks, seg_rows, taps_x[layer], taps_bc[layer]],
            [
                pltpu.VMEM((length, 256), BF),
                pltpu.VMEM((length, 256), BF),
                pltpu.VMEM((16, length), F32),
                pltpu.VMEM((length, 256), F32),
                pltpu.VMEM((length, 256), BF),
                pltpu.VMEM((length, 256), F32),
                pltpu.VMEM((length, 256), BF),
                pltpu.VMEM((length, 256), F32),
                pltpu.VMEM((16, length), F32),
                pltpu.VMEM((length, 128), F32),
                pltpu.VMEM((8, 128), F32),
                pltpu.VMEM((length, 256), BF),
                pltpu.VMEM((length, 256), F32),
                pltpu.VMEM((length, 256), F32),
                pltpu.VMEM((length, 256), F32),
                pltpu.VMEM((length, 128), F32),
                pltpu.VMEM((8, length), F32),
                pltpu.VMEM((length, 128), F32),
                pltpu.VMEM((length, 256), BF),
                pltpu.VMEM((length, 256), BF),
                pltpu.VMEM((16, length), BF),
            ],
            name="mix_back",
        )
        if waiting:
            (o0, o1, o2, o3), waiting = tied([o0, o1, o2, o3], waiting)
            waiting = [parity_sum(added(waiting[:4])), parity_sum(added(waiting[4:]))]
            waiting = [*across_heads([waiting[0]] * 4), transposed(waiting[1])]
        dmixed = across_tokens([o0, o1, o2, o3])
        if layer == layers - 1:
            dmixed, home = tied(dmixed, home)
        full_dzx, full_dside, gain_rows, *sent = local_call(
            in_back_body,
            [shape((256, wide), BF), shape((256, 256), BF), shape((8, width), F32),
             shape((64, width), F32)] + [shape((64, width), BF)] * 3,
            [place], [*dmixed, *in_weights[layer], bc_weight[layer], full_normed],
            [pltpu.VMEM((256, width), F32)] + [pltpu.VMEM((512, wide), BF)] * 2, name="in_back",
        )
        parts = across_heads(sent)
        smalls[layer] = transposed(
            copies_sum(jnp.concatenate([head_grads, small_grads], axis=0))
        )
        keep, give, keep_side, give_side = local_call(
            in_weight_body,
            [shape((512, wide), BF)] * 2 + [shape((576, 256), BF)] * 2,
            [place], [full_normed, full_dzx, full_dside, gain_rows, gains[layer], side_grads],
            [pltpu.VMEM((1024, wide), BF), pltpu.VMEM((1152, 256), BF)], name="in_weight",
        )
        if waiting:
            parts, waiting = tied(parts, waiting)
            arrived[layer + 1] = waiting
        parts, (keep, give, keep_side, give_side) = tied(
            parts, [keep, give, keep_side, give_side]
        )
        waiting = [
            keep_side, pair_swap(give_side), keep, pair_swap(give), keep_out, pair_swap(give_out)
        ]
        if layer > 0:
            mixed, inverse = kept[layer - 1][6:]
            grad, sent_grad = local_call(
                lambda *refs: back_middle_body(inner, *refs),
                [shape((64, width), F32), shape((64, wide), BF)],
                [], [*parts, grad, resid, scale, gains[layer], mixed, inverse],
                name="back_middle",
            )
        else:
            (final,) = local_call(
                back_end_body, [shape((64, width), BF)],
                [], [*parts, grad, resid, scale, gains[layer]], name="back_end",
            )
    waiting = side_messages(waiting)
    waiting = [*across_tokens(waiting[:4]), *across_tokens(waiting[4:])]
    waiting = [parity_sum(added(waiting[:4])), parity_sum(added(waiting[4:]))]
    arrived[0] = [*across_heads([waiting[0]] * 4), transposed(waiting[1])]
    for layer in reversed(range(layers)):
        *side, part = arrived[layer]
        (side,) = local_call(
            quarters_body, [shape((576, 256), BF)], [place], across_tokens([added(side)] * 4),
            name="quarters",
        )
        sides[layer] = (side, pair_swap(side))
        grads[layer] = (part, pair_swap(part))

    result_out, grad_out = local_call(
        place_body, [shape((256, width), BF), shape((256, width), F32)],
        [place], [*home, *across_heads([final] * 4)], name="place",
    )
    own_gain = jnp.broadcast_to(gnorm_gain[:, :, None], gnorm_gain.shape + (LANES,))
    order = list(range(layers))
    d_zx, d_dt, d_out, d_own, d_side, d_rest = local_call(
        lambda *refs: finish_body(layers, *refs),
        [
            shape((layers, 256, width), F32), shape((layers, 256, LANES), F32),
            shape((layers, 128, width), F32), shape((layers, 128, LANES), F32),
            shape((layers, width, 256), F32), shape((layers, 128, 256), F32),
        ],
        [place],
        [part for at in order for part in sides[at]]
        + [part for at in reversed(order) for part in grads[at]] + [own_gain],
        [pltpu.VMEM((1152, 256), F32)], name="finish",
    )
    small = jnp.stack(smalls)
    taps = small[:, :16].reshape(layers, 2, 8, LANES)[:, :, :5, 64:].transpose(0, 2, 1, 3)
    taps = taps.reshape(layers, 5, LANES)
    return (
        result_out, grad_out, d_rest[:, 0:4].reshape(layers, width), d_zx,
        d_dt[:, :, :heads_here], d_side, taps[:, :4], taps[:, 4],
        d_rest[:, 4:8], d_rest[:, 8], small[:, 16:18, 0], small[:, 16:18, 1], small[:, 16:18, 2],
        d_own[:, :, 0], d_out,
    )


def solution(mesh):
    placed = (
        P(("dp", "row"), None),
        P("dp", None),
        P(("dp", "row"), None),
        P(),
        P(None, "col", "row"),
        P(None, "col", "row"),
        P(),
        P(None, None, ("row", "col")),
        P(None, ("row", "col")),
        P(),
        P(),
        P(None, ("row", "col")),
        P(None, ("row", "col")),
        P(None, ("row", "col")),
        P(None, ("row", "col")),
        P(None, ("row", "col"), None),
    )
    return jax.shard_map(
        shards,
        mesh=mesh,
        in_specs=placed,
        out_specs=(
            P(("dp", "row"), None),
            P(("dp", "row"), None),
            P(),
            P(None, "col", "row"),
            P(None, "col", "row"),
            P(),
            P(None, None, ("row", "col")),
            P(None, ("row", "col")),
            P(),
            P(),
            P(None, ("row", "col")),
            P(None, ("row", "col")),
            P(None, ("row", "col")),
            P(None, ("row", "col")),
            P(None, ("row", "col"), None),
        ),
        check_vma=False,
    )
```
